128 devices in a mesh: tok: 8 (over z, core), feat: 16 (over x, y).
Axes of the slice: x: 4, y: 4, z: 4, core: 2. Of those that a mesh axis runs over, the one named last changes fastest.
Arguments:
- residual: bfloat16 [2, 2048, 3584], P(None, 'tok', 'feat'), may hold values from -6 to 6
- enc_weight: bfloat16 [2, 3584, 16384], P(None, None, 'feat'), may hold values from -0.09375 to 0.09375
- enc_bias: float32 [2, 16384], P(None, 'feat'), may hold values from -3 to 3
- dec_sum: bfloat16 [2, 16384, 3584], P(None, 'feat', 'tok'), may hold values from -0.09375 to 0.09375
- unembed: bfloat16 [131072, 3584], P(('tok', 'feat')), may hold values from -6 to 6
- norm_gain: float32 [3584], replicated, may hold values from 0.25 to 1.75
- target_ids: int32 [64], replicated, may hold values from 0 to 131071
- active_ids: int32 [2, 2048, 192], P(None, 'tok', 'feat'), may hold values from -1 to 16383, as said below
Outputs:
- edges: bfloat16 [2, 2048, 12288], P(None, ('tok', 'feat'))
The draws below stay inside these ranges and needn't reach their ends.
Inputs may be any that keep to these rules, and one draw needn't show every extreme that they name: `active_ids`: slot group g of a token and layer (slots g * 12 to (g + 1) * 12 - 1) holds distinct features of g * 1024 to (g + 1) * 1024 - 1 in its first slots, at least one, and -1 in the rest; in every layer some group is full.
All inputs are finite; a program needn't handle non-finite values.
Results may differ from the reference program's by a relative error of at most 0.0058.
Values may be sent and summed in bfloat16 or wider, within the bound.
No kernel may reach another device: no remote copies, remote signals or barrier semaphores. Data moves between devices by JAX's collectives and lax.ppermute only.
A program may use at most 128 MiB of HBM per device.

```python
import math
import jax
import jax.numpy as jnp
from jax import lax

D = 3584
F = 16384
L = 2
K = 192
NT = 64
TOKENS = 2048
VOCAB = 131072
FS = 1024
KS = 12


def draw_active_ids(key, part):
    base_key = jax.random.fold_in(key, 17)
    key_count, key_token, key_group, key_step, key_start = jax.random.split(base_key, 5)
    groups = K // KS
    counts = jax.random.randint(key_count, (L, TOKENS, groups), 1, max(2, 2 * KS // 3))
    full_token = jax.random.randint(key_token, (L, 1, 1), 0, TOKENS)
    full_group = jax.random.randint(key_group, (L, 1, 1), 0, groups)
    token_axis = jnp.arange(TOKENS, dtype=jnp.int32)[None, :, None]
    group_axis = jnp.arange(groups, dtype=jnp.int32)[None, None, :]
    counts = jnp.where((token_axis == full_token) & (group_axis == full_group), KS, counts)
    strides = jax.random.randint(key_step, (L, TOKENS, groups, KS), 1, max(2, FS // KS))
    starting = jax.random.randint(key_start, (L, TOKENS, groups, 1), 0, FS)
    within = (starting + jnp.cumsum(strides, axis=3) - strides) % FS
    features = within + group_axis[..., None] * FS
    slot_axis = jnp.arange(KS, dtype=jnp.int32)
    filled = slot_axis[None, None, None, :] < counts[..., None]
    return jnp.where(filled, features, -1).reshape(L, TOKENS, K).astype(jnp.int32)


def touch_ends(values, key, low, high):
    spot = [jax.random.randint(jax.random.fold_in(key, axis), (), 0, length) for axis, length in enumerate(values.shape)]
    longest = values.shape.index(max(values.shape))
    beside = spot[:longest] + [(spot[longest] + 1) % values.shape[longest]] + spot[longest + 1:]
    return values.at[tuple(spot)].set(low).at[tuple(beside)].set(high)


def level_of(own_key, dims, pieces, smallest, high):
    def one(dim, parts):
        draws = jax.random.uniform(jax.random.fold_in(jax.random.fold_in(own_key, 6), dim), (parts,), jnp.float32, smallest / len(pieces), high / len(pieces))
        return jnp.repeat(jnp.exp(draws), dims[dim] // parts).reshape((-1,) + (1,) * (len(dims) - dim - 1))

    gain = one(*pieces[0])
    for cut in pieces[1:]:
        gain = gain * one(*cut)
    return gain


def scatter_about(own_key, extent, width, most, shards=(), kind=jnp.bfloat16):
    values = jax.random.normal(own_key, extent, jnp.float32) * width
    if len(shards) > 0:
        values = level_of(own_key, extent, shards, -0.22, 0.18) * values
    return jnp.clip(values, min=-most, max=most).astype(kind)


def setup_inputs(seed: int = 0) -> dict:
    seeds = jax.random.split(jax.random.key(seed), 9)
    residual = scatter_about(seeds[0], (L, TOKENS, D), 1.0, 6.0, ((1, 8), (2, 16)))
    enc_weight = scatter_about(seeds[1], (L, D, F), D ** -0.5, 0.09375, ((2, 16),))
    enc_bias = scatter_about(seeds[2], (L, F), 0.5, 3.0, ((1, 16),), jnp.float32)
    dec_sum = scatter_about(seeds[3], (L, F, D), D ** -0.5, 0.09375, ((1, 16), (2, 8)))
    unembed = scatter_about(seeds[4], (VOCAB, D), 1.0, 6.0, ((0, 128),))
    norm_gain = jnp.clip(1.0 + 0.15 * jax.random.normal(seeds[5], (D,), jnp.float32), 0.25, 1.75)
    target_ids = touch_ends(jax.random.randint(seeds[6], (NT,), 0, VOCAB), jax.random.fold_in(seeds[6], 1), 0, VOCAB - 1).astype(jnp.int32)
    active_ids = draw_active_ids(jax.random.fold_in(seeds[8], 71), 0)
    return {"residual": residual, "enc_weight": enc_weight, "enc_bias": enc_bias, "dec_sum": dec_sum, "unembed": unembed, "norm_gain": norm_gain, "target_ids": target_ids, "active_ids": active_ids}


def reference(residual, enc_weight, enc_bias, dec_sum, unembed, norm_gain, target_ids, active_ids):
    target_rows = jnp.take(unembed, target_ids, axis=0).astype(jnp.float32)
    directions = (target_rows * norm_gain[None, :]).astype(jnp.bfloat16)
    block_rows = math.gcd(TOKENS, 64)
    results = []
    for layer_idx in range(L):
        scores = jnp.dot(dec_sum[layer_idx], directions.T, preferred_element_type=jnp.float32).astype(jnp.bfloat16)
        columns = enc_weight[layer_idx].T
        encoder_bias_rows = enc_bias[layer_idx]

        def one_block(operand_list, columns=columns, encoder_bias_rows=encoder_bias_rows, scores=scores):
            incoming_rows, feature_ids = operand_list
            is_live = feature_ids >= 0
            clipped_activation = jnp.where(is_live, feature_ids, jnp.zeros_like(feature_ids)).astype(jnp.int32)
            encoder_columns = jnp.take(columns, clipped_activation, axis=0).astype(jnp.float32)
            preactivation = jnp.einsum("jp,jlp->jl", incoming_rows.astype(jnp.float32), encoder_columns) + jnp.take(encoder_bias_rows, clipped_activation, axis=0)
            activation = jnp.where(is_live, preactivation, jnp.zeros_like(preactivation))
            picked = jnp.take(scores, clipped_activation, axis=0).astype(jnp.float32)
            edge_vals = (activation[:, :, None] * picked).astype(jnp.bfloat16)
            return edge_vals.reshape(edge_vals.shape[0], K * NT)

        blocks = lax.map(one_block, (residual[layer_idx].reshape(TOKENS // block_rows, block_rows, D),
                                     active_ids[layer_idx].reshape(TOKENS // block_rows, block_rows, K)))
        results.append(blocks.reshape(TOKENS, K * NT))
    return jnp.stack(results)
```

```python
import jax
import jax.numpy as jnp
from jax import lax
from jax.experimental import pallas as pl
from jax.experimental.pallas import tpu as pltpu
from jax.sharding import PartitionSpec as P


LANES = 128


def edge_kernel(steps, slots, targets, x_ref, w_ref, bias_ref, loc_ref, table_ref, out_ref, acc_ref):
    step = pl.program_id(1)
    product = lax.dot_general(
        x_ref[0], w_ref[0], (((0,), (0,)), ((), ())), preferred_element_type=jnp.float32
    )

    @pl.when(step == 0)
    def _():
        acc_ref[...] = product + bias_ref[0]

    @pl.when(step > 0)
    def _():
        acc_ref[...] += product

    @pl.when(step == steps - 1)
    def _():
        rows, feats = acc_ref.shape
        loc = loc_ref[0]
        lane = lax.broadcasted_iota(jnp.int32, (rows, LANES), 1)
        lo = loc & (LANES - 1)
        group = loc >> 7
        act = jnp.zeros((rows, LANES), jnp.float32)
        for g in range(feats // LANES):
            got = jnp.take_along_axis(acc_ref[:, g * LANES:(g + 1) * LANES], lo, axis=1)
            act = jnp.where(group == g, got, act)
        width = 2 * LANES
        n_hi = feats // width
        table = table_ref[0]
        blank = jnp.zeros((targets, width), table.dtype)
        even, odd = [], []
        for h in range(n_hi):
            part = table[:, h * width:(h + 1) * width]
            even += [part, blank]
            odd += [blank, part]
        rhs = jnp.concatenate([jnp.concatenate(even, 0), jnp.concatenate(odd, 0)], 1)
        for j in range(slots // 2):
            halves = []
            for k in (2 * j, 2 * j + 1):
                here = jnp.take_along_axis(loc, jnp.full((rows, LANES), k, jnp.int32), axis=1)
                low = here & (width - 1)
                for part in range(2):
                    halves.append(
                        jnp.where(low == lane + part * LANES, 1.0, 0.0).astype(table.dtype)
                    )
            onehot = jnp.concatenate(halves, 1)
            found = lax.dot_general(
                onehot, rhs, (((1,), (1,)), ((), ())), preferred_element_type=jnp.float32
            )
            spread = 2 * j + (lane >> 6)
            hi = jnp.take_along_axis(loc, spread, axis=1) >> 8
            value = jnp.take_along_axis(act, spread, axis=1)
            picked = jnp.zeros((rows, LANES), jnp.float32)
            for h in range(n_hi):
                picked = jnp.where(hi == h, found[:, h * LANES:(h + 1) * LANES], picked)
            edges = (value * picked).astype(out_ref.dtype)
            parts = out_ref.shape[0]
            out_ref[:, 0, :, j * LANES:(j + 1) * LANES] = edges.reshape(parts, rows // parts, LANES)


def make_edges(x, weight, bias, loc, table, parts):
    layers, depth, rows = x.shape
    feats = weight.shape[2]
    targets = table.shape[1]
    slots = 12
    block = 512
    steps = depth // block
    kernel = lambda *refs: edge_kernel(steps, slots, targets, *refs)
    return pl.pallas_call(
        kernel,
        grid=(layers, steps),
        in_specs=[
            pl.BlockSpec((1, block, rows), lambda l, s: (l, s, 0)),
            pl.BlockSpec((1, block, feats), lambda l, s: (l, s, 0)),
            pl.BlockSpec((1, 1, feats), lambda l, s: (l, 0, 0)),
            pl.BlockSpec((1, rows, LANES), lambda l, s: (l, 0, 0)),
            pl.BlockSpec((1, targets, feats), lambda l, s: (l, 0, 0)),
        ],
        out_specs=pl.BlockSpec((parts, 1, rows // parts, slots * targets), lambda l, s: (0, l, 0, 0)),
        out_shape=jax.ShapeDtypeStruct((parts, layers, rows // parts, slots * targets), jnp.bfloat16),
        scratch_shapes=[pltpu.VMEM((rows, feats), jnp.float32)],
        compiler_params=pltpu.CompilerParams(
            dimension_semantics=("arbitrary", "arbitrary"), vmem_limit_bytes=40 * 2**20
        ),
        cost_estimate=pl.CostEstimate(
            flops=2 * layers * rows * depth * feats,
            bytes_accessed=2 * layers * depth * (feats + rows),
            transcendentals=0,
        ),
        name="edges",
    )(x, weight, bias, loc, table)


def partner_of(axis, flip):
    pairs = []
    for i in range(128):
        tok, feat = divmod(i, 16)
        place = {"z": tok // 2, "core": tok % 2, "x": feat // 4, "y": feat % 4}
        place[axis] ^= flip
        pairs.append((i, (place["z"] * 2 + place["core"]) * 16 + place["x"] * 4 + place["y"]))
    return pairs


def swap(value, axis, flip):
    return lax.ppermute(value, ("tok", "feat"), partner_of(axis, flip))


def at(value, i):
    return lax.dynamic_index_in_dim(value, i, 0, keepdims=False)


def per_device(residual, enc_weight, enc_bias, dec_sum, unembed, norm_gain, target_ids, active_ids):
    n_feat = lax.axis_size("feat")
    feat_pos = lax.axis_index("feat")
    tok_pos = lax.axis_index("tok")
    z, core = tok_pos // 2, tok_pos % 2
    layers, rows, depth_part = residual.shape
    feat_rows = enc_weight.shape[2]
    targets = target_ids.shape[0]
    width_part = dec_sum.shape[2]

    x = lax.all_gather(residual.transpose(0, 2, 1), "feat", axis=1, tiled=True)

    vocab_rows = unembed.shape[0]
    first_row = (tok_pos * n_feat + feat_pos) * vocab_rows
    selector = (
        target_ids[:, None] - first_row == jnp.arange(vocab_rows, dtype=jnp.int32)[None, :]
    ).astype(jnp.bfloat16)
    own_rows = jnp.dot(selector, unembed, preferred_element_type=jnp.float32)
    own = (own_rows * norm_gain[None, :]).astype(jnp.bfloat16)
    own = own.reshape(targets, 4, 2, width_part).transpose(2, 1, 0, 3)
    mine = at(own, core) + swap(at(own, 1 - core), "core", 1)
    keep = jnp.stack([at(mine, z), at(mine, z ^ 1)])
    give = jnp.stack([at(mine, z ^ 3), at(mine, z ^ 2)])
    keep = keep + swap(give, "z", 3)
    part = keep[0] + swap(keep[1], "z", 1)
    for axis, flip in (("x", 1), ("x", 3), ("y", 1), ("y", 3)):
        part = part + swap(part, axis, flip)

    terms = jnp.einsum("td,lfd->ltf", part, dec_sum, preferred_element_type=jnp.float32)
    total = at(terms, core) + swap(at(terms, 1 - core), "core", 1)
    for flip in (3, 1):
        total = total + swap(total.astype(jnp.bfloat16), "z", flip).astype(jnp.float32)
    mine = total.astype(jnp.bfloat16)
    theirs = swap(mine, "core", 1)
    table = jnp.stack([jnp.where(core == 0, mine, theirs), jnp.where(core == 0, theirs, mine)])

    loc = jnp.where(active_ids >= 0, active_ids - feat_pos * feat_rows, -1)
    slots = loc.shape[2]
    loc = jnp.pad(loc, ((0, 0), (0, 0), (0, LANES - slots)), constant_values=-1)
    edges = make_edges(x, enc_weight, enc_bias[:, None, :], loc, table, n_feat)
    edges = lax.all_to_all(edges, "feat", split_axis=0, concat_axis=0, tiled=True)
    return edges.transpose(1, 2, 0, 3).reshape(layers, rows // n_feat, n_feat * slots * targets)


def solution(mesh):
    return jax.shard_map(
        per_device,
        mesh=mesh,
        in_specs=(
            P(None, "tok", "feat"),
            P(None, None, "feat"),
            P(None, "feat"),
            P(None, "feat", "tok"),
            P(("tok", "feat"), None),
            P(),
            P(),
            P(None, "tok", "feat"),
        ),
        out_specs=P(None, ("tok", "feat"), None),
        check_vma=False,
    )
```

```python
import jax
import jax.numpy as jnp
from jax import lax
from jax.experimental import pallas as pl
from jax.experimental.pallas import tpu as pltpu
from jax.sharding import PartitionSpec as P


LANES = 128
CHUNKS = ((4, 4, 8), (8, 8))
X_PIECE = 4
W_PIECE = 2
AHEAD = 12
EDGE_VMEM = 56 * 2**20
ROWS_VMEM = 60 * 2**20


def owned_rows_kernel(place_ref, ids_ref, unembed_hbm, gain_ref, keep_ref, send_ref, tile_buf, row_buf, sem):
    targets = ids_ref.shape[0]
    tile = tile_buf.shape[1]
    first, count, z, core = place_ref[0], unembed_hbm.shape[0], place_ref[1], place_ref[2]

    def copy(i):
        row = ids_ref[i] - first
        start = pl.multiple_of(lax.shift_right_logical(row, 3) * tile, tile)
        return pltpu.make_async_copy(unembed_hbm.at[pl.ds(start, tile)], tile_buf.at[i], sem.at[i])

    def is_owned(i):
        row = ids_ref[i] - first
        return jnp.logical_and(row >= 0, row < count)

    @pl.loop(0, targets)
    def _(i):
        @pl.when(is_owned(i))
        def _():
            copy(i).start()

    row_buf[...] = jnp.zeros_like(row_buf)

    @pl.loop(0, targets)
    def _(i):
        @pl.when(is_owned(i))
        def _():
            copy(i).wait()
            rows = tile_buf[i].astype(jnp.float32)
            wanted = (ids_ref[i] - first) & (tile - 1)
            here = lax.broadcasted_iota(jnp.int32, rows.shape, 0) == wanted
            row = jnp.sum(jnp.where(here, rows, 0.0), axis=0, keepdims=True)
            row_buf[pl.ds(i, 1), :] = row * gain_ref[...]

    zs, _, width = keep_ref.shape
    for part in range(2 * zs):
        value = row_buf[:, part * width:(part + 1) * width].astype(keep_ref.dtype)
        slot = z ^ (part // 2)

        @pl.when(core == part % 2)
        def _(value=value, slot=slot):
            keep_ref[slot] = value

        @pl.when(core != part % 2)
        def _(value=value, slot=slot):
            send_ref[slot] = value


def owned_rows(place, target_ids, unembed, gain, parts):
    targets = target_ids.shape[0]
    depth = unembed.shape[1]
    smem = pl.BlockSpec(memory_space=pltpu.SMEM)
    vmem = pl.BlockSpec(memory_space=pltpu.VMEM)
    shape = jax.ShapeDtypeStruct((parts // 2, targets, depth // parts), jnp.bfloat16)
    return pl.pallas_call(
        owned_rows_kernel,
        in_specs=[smem, smem, pl.BlockSpec(memory_space=pl.ANY), vmem],
        out_specs=[vmem, vmem],
        out_shape=[shape, shape],
        scratch_shapes=[
            pltpu.VMEM((targets, 8, depth), unembed.dtype),
            pltpu.VMEM((targets, depth), jnp.float32),
            pltpu.SemaphoreType.DMA((targets,)),
        ],
        compiler_params=pltpu.CompilerParams(vmem_limit_bytes=ROWS_VMEM),
        name="owned_rows",
    )(place, target_ids, unembed, gain)


def edge_kernel(place_ref, x_hbm, w_hbm, bias_ref, ids_ref, mine_ref, theirs_ref, out_ref, x_buf, w_buf, acc_ref, ids_buf, x_sem, w_sem):
    layers, blocks, block, rows = x_buf.shape
    depth, feats = w_buf.shape[1:]
    slots = ids_ref.shape[1]
    targets = mine_ref.shape[0]
    core, first = place_ref[2], place_ref[3]

    def x_copy(layer, piece):
        part = pl.ds(piece * X_PIECE, X_PIECE)
        return pltpu.make_async_copy(x_hbm.at[part, layer], x_buf.at[layer, part], x_sem.at[layer, piece])

    def w_copy(layer, piece):
        part = pl.ds(piece * W_PIECE * block, W_PIECE * block)
        return pltpu.make_async_copy(w_hbm.at[layer, part], w_buf.at[layer, part], w_sem.at[layer, piece])

    queue, needs = [], []
    for layer in range(layers):
        done_x = done_w = 0
        for chunk in range(len(CHUNKS[layer])):
            end = sum(CHUNKS[layer][:chunk + 1])
            need = []
            while done_x * X_PIECE < end:
                need.append(x_copy(layer, done_x))
                done_x += 1
            while done_w * W_PIECE < end:
                need.append(w_copy(layer, done_w))
                done_w += 1
            queue += need
            needs.append(need)

    def start_next():
        if queue:
            queue.pop(0).start()

    for _ in range(AHEAD):
        start_next()

    lane = lax.broadcasted_iota(jnp.int32, (rows, LANES), 1)
    lower = lane < targets
    width = 2 * LANES
    for layer in range(layers):
        for chunk, count in enumerate(CHUNKS[layer]):
            for copy in needs.pop(0):
                copy.wait()
                start_next()
            start = sum(CHUNKS[layer][:chunk])
            product = lax.dot_general(
                x_buf[layer, start:start + count].reshape(count * block, rows),
                w_buf[layer, start * block:(start + count) * block],
                (((0,), (0,)), ((), ())),
                preferred_element_type=jnp.float32,
            )
            if chunk == 0:
                acc_ref[...] = product + bias_ref[layer:layer + 1, :]
            else:
                acc_ref[...] += product

        ids_buf[...] = jnp.full_like(ids_buf, -1)
        ids_buf[:slots, :] = ids_ref[layer]
        ids = ids_buf[...].T
        loc = jnp.where(ids >= 0, ids - first, -1)
        lo = loc & (LANES - 1)
        group = loc >> 7
        act = jnp.zeros((rows, LANES), jnp.float32)
        for g in range(feats // LANES):
            got = jnp.take_along_axis(acc_ref[:, g * LANES:(g + 1) * LANES], lo, axis=1)
            act = jnp.where(group == g, got, act)
        table = jnp.where(core == layer, mine_ref[...], theirs_ref[...])
        rhs = jnp.concatenate([table[:, h * width:(h + 1) * width] for h in range(feats // width)], 0)
        for j in range(slots // 2):
            halves = []
            for k in (2 * j, 2 * j + 1):
                here = jnp.take_along_axis(loc, jnp.full((rows, LANES), k, jnp.int32), axis=1)
                low = here & (width - 1)
                onehot = jnp.concatenate(
                    [jnp.where(low == lane + part * LANES, 1.0, 0.0).astype(table.dtype) for part in range(2)], 1
                )
                found = lax.dot_general(
                    onehot, rhs, (((1,), (1,)), ((), ())), preferred_element_type=jnp.float32
                )
                quarter = here >> 8
                two = jnp.where(quarter < 2, found[:, :LANES], found[:, LANES:])
                turned = pltpu.roll(two, targets, 1)
                halves.append(jnp.where((quarter & 1) == k % 2, two, turned))
            picked = jnp.where(lower, halves[0], halves[1])
            value = jnp.take_along_axis(act, 2 * j + (lane >> 6), axis=1)
            edges = (value * picked).astype(out_ref.dtype)
            parts = out_ref.shape[0]
            out_ref[:, layer, :, j * LANES:(j + 1) * LANES] = edges.reshape(parts, rows // parts, LANES)


def make_edges(place, x, weight, bias, ids, mine, theirs):
    blocks, layers, block, rows = x.shape
    depth, feats = weight.shape[1:]
    slots = ids.shape[1]
    targets = mine.shape[0]
    smem = pl.BlockSpec(memory_space=pltpu.SMEM)
    vmem = pl.BlockSpec(memory_space=pltpu.VMEM)
    hbm = pl.BlockSpec(memory_space=pl.ANY)
    return pl.pallas_call(
        edge_kernel,
        in_specs=[smem, hbm, hbm, vmem, vmem, vmem, vmem],
        out_specs=vmem,
        out_shape=jax.ShapeDtypeStruct((blocks, layers, rows // blocks, slots * targets), jnp.bfloat16),
        scratch_shapes=[
            pltpu.VMEM((layers, blocks, block, rows), x.dtype),
            pltpu.VMEM((layers, depth, feats), weight.dtype),
            pltpu.VMEM((rows, feats), jnp.float32),
            pltpu.VMEM((LANES, rows), jnp.int32),
            pltpu.SemaphoreType.DMA((layers, blocks // X_PIECE)),
            pltpu.SemaphoreType.DMA((layers, blocks // W_PIECE)),
        ],
        compiler_params=pltpu.CompilerParams(vmem_limit_bytes=EDGE_VMEM),
        cost_estimate=pl.CostEstimate(
            flops=2 * layers * rows * depth * feats,
            bytes_accessed=2 * layers * depth * (feats + rows),
            transcendentals=0,
        ),
        name="edges",
    )(place, x, weight, bias, ids, mine, theirs)


def partner_of(axis, flip):
    pairs = []
    for i in range(128):
        tok, feat = divmod(i, 16)
        place = {"z": tok // 2, "core": tok % 2, "x": feat // 4, "y": feat % 4}
        place[axis] ^= flip
        pairs.append((i, (place["z"] * 2 + place["core"]) * 16 + place["x"] * 4 + place["y"]))
    return pairs


def swap(value, axis, flip):
    return lax.ppermute(value, ("tok", "feat"), partner_of(axis, flip))


def per_device(residual, enc_weight, enc_bias, dec_sum, unembed, norm_gain, target_ids, active_ids):
    n_tok = lax.axis_size("tok")
    n_feat = lax.axis_size("feat")
    feat_pos = lax.axis_index("feat")
    tok_pos = lax.axis_index("tok")
    z, core = tok_pos // 2, tok_pos % 2
    layers, rows, _ = residual.shape
    feat_rows = enc_weight.shape[2]
    targets = target_ids.shape[0]
    slots = active_ids.shape[2]

    x = lax.all_gather(residual.transpose(0, 2, 1), "feat", axis=0, tiled=False)

    first_row = (tok_pos * n_feat + feat_pos) * unembed.shape[0]
    place = jnp.stack([first_row, z, core, feat_pos * feat_rows])
    keep, send = owned_rows(place, target_ids, unembed, norm_gain[None, :], n_tok)
    keep = keep + swap(send, "core", 1)
    keep = keep[:2] + swap(keep[:1:-1], "z", 3)
    part = keep[0] + swap(keep[1], "z", 1)
    for axis, flip in (("x", 1), ("x", 3), ("y", 1), ("y", 3)):
        part = part + swap(part, axis, flip)

    terms = jnp.einsum("td,lfd->ltf", part, dec_sum, preferred_element_type=jnp.float32)
    own = lax.dynamic_index_in_dim(terms, core, 0, keepdims=False)
    other = lax.dynamic_index_in_dim(terms, 1 - core, 0, keepdims=False)
    total = own + swap(other, "core", 1)
    for flip in (3, 1):
        total = total + swap(total.astype(jnp.bfloat16), "z", flip).astype(jnp.float32)
    mine = total.astype(jnp.bfloat16)
    theirs = swap(mine, "core", 1)

    edges = make_edges(place, x, enc_weight, enc_bias, active_ids.transpose(0, 2, 1), mine, theirs)
    edges = lax.all_to_all(edges, "feat", split_axis=0, concat_axis=0, tiled=True)
    return edges.transpose(1, 2, 0, 3).reshape(layers, rows // n_feat, n_feat * slots * targets)


def solution(mesh):
    return jax.shard_map(
        per_device,
        mesh=mesh,
        in_specs=(
            P(None, "tok", "feat"),
            P(None, None, "feat"),
            P(None, "feat"),
            P(None, "feat", "tok"),
            P(("tok", "feat"), None),
            P(),
            P(),
            P(None, "tok", "feat"),
        ),
        out_specs=P(None, ("tok", "feat"), None),
        check_vma=False,
    )
```

```python
import jax
import jax.numpy as jnp
from jax import lax
from jax.experimental import pallas as pl
from jax.experimental.pallas import tpu as pltpu
from jax.sharding import PartitionSpec as P


LANES = 128
CHUNKS = ((4, 4, 8), (8, 8))
X_PIECE = 4
W_PIECE = 2
AHEAD = 12
FEATS = 1024
EDGE_VMEM = 56 * 2**20
PICK_VMEM = 24 * 2**20
ROWS_VMEM = 60 * 2**20


def owned_rows_kernel(ids_ref, unembed_hbm, gain_ref, keep_ref, send_ref, tile_buf, row_buf, sem):
    targets = ids_ref.shape[0]
    tile = tile_buf.shape[1]
    count = unembed_hbm.shape[0]
    tok = lax.axis_index("tok")
    first = (tok * lax.axis_size("feat") + lax.axis_index("feat")) * count
    z, core = tok // 2, tok % 2

    def copy(i):
        row = ids_ref[i] - first
        start = pl.multiple_of(lax.shift_right_logical(row, 3) * tile, tile)
        return pltpu.make_async_copy(unembed_hbm.at[pl.ds(start, tile)], tile_buf.at[i], sem.at[i])

    def is_owned(i):
        row = ids_ref[i] - first
        return jnp.logical_and(row >= 0, row < count)

    @pl.loop(0, targets, unroll=8)
    def _(i):
        @pl.when(is_owned(i))
        def _():
            copy(i).start()

    row_buf[...] = jnp.zeros_like(row_buf)

    gain = gain_ref[...].reshape(1, row_buf.shape[1])

    @pl.loop(0, targets, unroll=8)
    def _(i):
        @pl.when(is_owned(i))
        def _():
            copy(i).wait()
            rows = tile_buf[i].astype(jnp.float32)
            wanted = (ids_ref[i] - first) & (tile - 1)
            here = lax.broadcasted_iota(jnp.int32, rows.shape, 0) == wanted
            row = jnp.sum(jnp.where(here, rows, 0.0), axis=0, keepdims=True)
            row_buf[pl.ds(i, 1), :] = row * gain

    zs, _, width = keep_ref.shape
    for part in range(2 * zs):
        value = row_buf[:, part * width:(part + 1) * width].astype(keep_ref.dtype)
        slot = z ^ (part // 2)

        @pl.when(core == part % 2)
        def _(value=value, slot=slot):
            keep_ref[slot] = value

        @pl.when(core != part % 2)
        def _(value=value, slot=slot):
            send_ref[slot] = value


def owned_rows(target_ids, unembed, gain, parts):
    targets = target_ids.shape[0]
    depth = unembed.shape[1]
    smem = pl.BlockSpec(memory_space=pltpu.SMEM)
    vmem = pl.BlockSpec(memory_space=pltpu.VMEM)
    shape = jax.ShapeDtypeStruct((parts // 2, targets, depth // parts), jnp.bfloat16)
    return pl.pallas_call(
        owned_rows_kernel,
        in_specs=[smem, pl.BlockSpec(memory_space=pl.ANY), vmem],
        out_specs=[vmem, vmem],
        out_shape=[shape, shape],
        scratch_shapes=[
            pltpu.VMEM((targets, 8, depth), unembed.dtype),
            pltpu.VMEM((targets, depth), jnp.float32),
            pltpu.SemaphoreType.DMA((targets,)),
        ],
        compiler_params=pltpu.CompilerParams(vmem_limit_bytes=ROWS_VMEM),
        name="owned_rows",
    )(target_ids, unembed, gain)


def edge_kernel(x_hbm, w_hbm, bias_ref, ids_ref, picked_ref, out_ref, x_buf, w_buf, acc_ref, ids_buf, x_sem, w_sem):
    layers, blocks, block, rows = x_buf.shape
    depth, feats = w_buf.shape[1:]
    slots = ids_ref.shape[0]

    def x_copy(layer, piece):
        part = pl.ds(piece * X_PIECE, X_PIECE)
        return pltpu.make_async_copy(x_hbm.at[part, layer], x_buf.at[layer, part], x_sem.at[layer, piece])

    def w_copy(layer, piece):
        part = pl.ds(piece * W_PIECE * block, W_PIECE * block)
        return pltpu.make_async_copy(w_hbm.at[layer, part], w_buf.at[layer, part], w_sem.at[layer, piece])

    queue, needs = [], []
    for layer in range(layers):
        done_x = done_w = 0
        for chunk in range(len(CHUNKS[layer])):
            end = sum(CHUNKS[layer][:chunk + 1])
            need = []
            while done_x * X_PIECE < end:
                need.append(x_copy(layer, done_x))
                done_x += 1
            while done_w * W_PIECE < end:
                need.append(w_copy(layer, done_w))
                done_w += 1
            queue += need
            needs.append(need)

    def start_next():
        if queue:
            queue.pop(0).start()

    for _ in range(AHEAD):
        start_next()

    lane = lax.broadcasted_iota(jnp.int32, (rows, LANES), 1)
    for layer in range(layers):
        for chunk, count in enumerate(CHUNKS[layer]):
            for copy in needs.pop(0):
                copy.wait()
                start_next()
            start = sum(CHUNKS[layer][:chunk])
            product = lax.dot_general(
                x_buf[layer, start:start + count].reshape(count * block, rows),
                w_buf[layer, start * block:(start + count) * block],
                (((0,), (0,)), ((), ())),
                preferred_element_type=jnp.float32,
            )
            if chunk == 0:
                acc_ref[...] = product + bias_ref[layer:layer + 1, :]
            else:
                acc_ref[...] += product

        loc = local_slots(ids_ref, ids_buf, layer)
        lo = loc & (LANES - 1)
        group = loc >> 7
        act = jnp.zeros((rows, LANES), jnp.float32)
        for g in range(feats // LANES):
            got = jnp.take_along_axis(acc_ref[:, g * LANES:(g + 1) * LANES], lo, axis=1)
            act = jnp.where(group == g, got, act)
        for j in range(slots // 2):
            columns = slice(j * LANES, (j + 1) * LANES)
            value = jnp.take_along_axis(act, 2 * j + (lane >> 6), axis=1)
            edges = (value * picked_ref[layer, :, columns].astype(jnp.float32)).astype(out_ref.dtype)
            out_ref[:, layer, :, columns] = edges.reshape(blocks, rows // blocks, LANES)


def local_slots(ids_ref, ids_buf, layer):
    slots = ids_ref.shape[0]
    ids_buf[...] = jnp.full_like(ids_buf, -1)
    ids_buf[:slots, :] = ids_ref[:, layer, :]
    ids = ids_buf[...].T
    return jnp.where(ids >= 0, ids - lax.axis_index("feat") * FEATS, -1)


def pick_kernel(ids_ref, mine_ref, theirs_ref, picked_ref, ids_buf):
    slots, layers, rows = ids_ref.shape
    targets, feats = mine_ref.shape
    core = lax.axis_index("tok") % 2
    lane = lax.broadcasted_iota(jnp.int32, (rows, LANES), 1)
    lower = lane < targets
    width = 2 * LANES
    for layer in range(layers):
        loc = local_slots(ids_ref, ids_buf, layer)
        table = jnp.where(core == layer, mine_ref[...], theirs_ref[...])
        rhs = jnp.concatenate([table[:, h * width:(h + 1) * width] for h in range(feats // width)], 0)
        for j in range(slots // 2):
            halves = []
            for k in (2 * j, 2 * j + 1):
                here = jnp.take_along_axis(loc, jnp.full((rows, LANES), k, jnp.int32), axis=1)
                low = here & (width - 1)
                onehot = jnp.concatenate(
                    [jnp.where(low == lane + part * LANES, 1.0, 0.0).astype(table.dtype) for part in range(2)], 1
                )
                found = lax.dot_general(
                    onehot, rhs, (((1,), (1,)), ((), ())), preferred_element_type=jnp.float32
                )
                quarter = here >> 8
                two = jnp.where(quarter < 2, found[:, :LANES], found[:, LANES:])
                turned = pltpu.roll(two, targets, 1)
                halves.append(jnp.where((quarter & 1) == k % 2, two, turned))
            picked = jnp.where(lower, halves[0], halves[1])
            picked_ref[layer, :, j * LANES:(j + 1) * LANES] = picked.astype(picked_ref.dtype)


def pick_scores(ids, mine, theirs):
    slots, layers, rows = ids.shape
    targets = mine.shape[0]
    vmem = pl.BlockSpec(memory_space=pltpu.VMEM)
    return pl.pallas_call(
        pick_kernel,
        in_specs=[vmem, vmem, vmem],
        out_specs=vmem,
        out_shape=jax.ShapeDtypeStruct((layers, rows, slots * targets), mine.dtype),
        scratch_shapes=[pltpu.VMEM((LANES, rows), jnp.int32)],
        compiler_params=pltpu.CompilerParams(vmem_limit_bytes=PICK_VMEM),
        name="pick_scores",
    )(ids, mine, theirs)


def make_edges(x, weight, bias, ids, picked):
    blocks, layers, block, rows = x.shape
    depth, feats = weight.shape[1:]
    vmem = pl.BlockSpec(memory_space=pltpu.VMEM)
    hbm = pl.BlockSpec(memory_space=pl.ANY)
    return pl.pallas_call(
        edge_kernel,
        in_specs=[hbm, hbm, vmem, vmem, vmem],
        out_specs=vmem,
        out_shape=jax.ShapeDtypeStruct((blocks, layers, rows // blocks, picked.shape[2]), jnp.bfloat16),
        scratch_shapes=[
            pltpu.VMEM((layers, blocks, block, rows), x.dtype),
            pltpu.VMEM((layers, depth, feats), weight.dtype),
            pltpu.VMEM((rows, feats), jnp.float32),
            pltpu.VMEM((LANES, rows), jnp.int32),
            pltpu.SemaphoreType.DMA((layers, blocks // X_PIECE)),
            pltpu.SemaphoreType.DMA((layers, blocks // W_PIECE)),
        ],
        compiler_params=pltpu.CompilerParams(vmem_limit_bytes=EDGE_VMEM),
        cost_estimate=pl.CostEstimate(
            flops=2 * layers * rows * depth * feats,
            bytes_accessed=2 * layers * depth * (feats + rows),
            transcendentals=0,
        ),
        name="edges",
    )(x, weight, bias, ids, picked)


def partner_of(axis, flip):
    pairs = []
    for i in range(128):
        tok, feat = divmod(i, 16)
        place = {"z": tok // 2, "core": tok % 2, "x": feat // 4, "y": feat % 4}
        place[axis] ^= flip
        pairs.append((i, (place["z"] * 2 + place["core"]) * 16 + place["x"] * 4 + place["y"]))
    return pairs


def swap(value, axis, flip):
    return lax.ppermute(value, ("tok", "feat"), partner_of(axis, flip))


def per_device(residual, enc_weight, enc_bias, dec_sum, unembed, norm_gain, target_ids, active_ids):
    n_tok = lax.axis_size("tok")
    n_feat = lax.axis_size("feat")
    tok_pos = lax.axis_index("tok")
    core = tok_pos % 2
    layers, rows, _ = residual.shape
    targets = target_ids.shape[0]
    slots = active_ids.shape[2]

    x = lax.all_gather(residual.transpose(0, 2, 1), "feat", axis=0, tiled=False)

    keep, send = owned_rows(target_ids, unembed, norm_gain, n_tok)
    keep = keep + swap(send, "core", 1)
    keep = keep[:2] + swap(keep[:1:-1], "z", 3)
    part = keep[0] + swap(keep[1], "z", 1)
    for axis, flip in (("x", 1), ("x", 3), ("y", 1), ("y", 3)):
        part = part + swap(part, axis, flip)

    terms = jnp.einsum("td,lfd->ltf", part, dec_sum, preferred_element_type=jnp.float32)
    own = lax.dynamic_index_in_dim(terms, core, 0, keepdims=False)
    other = lax.dynamic_index_in_dim(terms, 1 - core, 0, keepdims=False)
    total = own + swap(other, "core", 1)
    for flip in (3, 1):
        total = total + swap(total.astype(jnp.bfloat16), "z", flip).astype(jnp.float32)
    mine = total.astype(jnp.bfloat16)
    theirs = swap(mine, "core", 1)

    ids = active_ids.transpose(2, 0, 1)
    edges = make_edges(x, enc_weight, enc_bias, ids, pick_scores(ids, mine, theirs))
    edges = lax.all_to_all(edges, "feat", split_axis=0, concat_axis=0, tiled=True)
    return edges.transpose(1, 2, 0, 3).reshape(layers, rows // n_feat, n_feat * slots * targets)


def solution(mesh):
    return jax.shard_map(
        per_device,
        mesh=mesh,
        in_specs=(
            P(None, "tok", "feat"),
            P(None, None, "feat"),
            P(None, "feat"),
            P(None, "feat", "tok"),
            P(("tok", "feat"), None),
            P(),
            P(),
            P(None, "tok", "feat"),
        ),
        out_specs=P(None, ("tok", "feat"), None),
        check_vma=False,
    )
```

```python
import jax
import jax.numpy as jnp
from jax import lax
from jax.experimental import pallas as pl
from jax.experimental.pallas import tpu as pltpu
from jax.sharding import PartitionSpec as P


LANES = 128
CHUNKS = ((4, 4, 8), (8, 8))
X_PIECE = 4
W_PIECE = 4
AHEAD = 16
PICKS = ((0,), (1,), ())
FEATS = 1024
EDGE_VMEM = 52 * 2**20
ROWS_VMEM = 50 * 2**20


def owned_rows_kernel(ids_ref, unembed_hbm, gain_ref, keep_ref, send_ref, tile_buf, row_buf, sem):
    targets = ids_ref.shape[0]
    tile = tile_buf.shape[1]
    count = unembed_hbm.shape[0]
    tok = lax.axis_index("tok")
    first = (tok * lax.axis_size("feat") + lax.axis_index("feat")) * count
    z, core = tok // 2, tok % 2

    def copy(i):
        row = ids_ref[i] - first
        start = pl.multiple_of(lax.shift_right_logical(row, 3) * tile, tile)
        return pltpu.make_async_copy(unembed_hbm.at[pl.ds(start, tile)], tile_buf.at[i], sem.at[i])

    def is_owned(i):
        row = ids_ref[i] - first
        return jnp.logical_and(row >= 0, row < count)

    @pl.loop(0, targets, unroll=8)
    def _(i):
        @pl.when(is_owned(i))
        def _():
            copy(i).start()

    row_buf[...] = jnp.zeros_like(row_buf)

    gain = gain_ref[...].reshape(1, row_buf.shape[1])

    @pl.loop(0, targets, unroll=8)
    def _(i):
        @pl.when(is_owned(i))
        def _():
            copy(i).wait()
            rows = tile_buf[i].astype(jnp.float32)
            wanted = (ids_ref[i] - first) & (tile - 1)
            here = lax.broadcasted_iota(jnp.int32, rows.shape, 0) == wanted
            row = jnp.sum(jnp.where(here, rows, 0.0), axis=0, keepdims=True)
            row_buf[pl.ds(i, 1), :] = row * gain

    zs, _, width = keep_ref.shape
    for part in range(2 * zs):
        value = row_buf[:, part * width:(part + 1) * width].astype(keep_ref.dtype)
        slot = z ^ (part // 2)

        @pl.when(core == part % 2)
        def _(value=value, slot=slot):
            keep_ref[slot] = value

        @pl.when(core != part % 2)
        def _(value=value, slot=slot):
            send_ref[slot] = value


def owned_rows(target_ids, unembed, gain, parts):
    targets = target_ids.shape[0]
    depth = unembed.shape[1]
    smem = pl.BlockSpec(memory_space=pltpu.SMEM)
    vmem = pl.BlockSpec(memory_space=pltpu.VMEM)
    shape = jax.ShapeDtypeStruct((parts // 2, targets, depth // parts), jnp.bfloat16)
    return pl.pallas_call(
        owned_rows_kernel,
        in_specs=[smem, pl.BlockSpec(memory_space=pl.ANY), vmem],
        out_specs=[vmem, vmem],
        out_shape=[shape, shape],
        scratch_shapes=[
            pltpu.VMEM((targets, 8, depth), unembed.dtype),
            pltpu.VMEM((targets, depth), jnp.float32),
            pltpu.SemaphoreType.DMA((targets,)),
        ],
        compiler_params=pltpu.CompilerParams(vmem_limit_bytes=ROWS_VMEM),
        name="owned_rows",
    )(target_ids, unembed, gain)


def edge_kernel(
    x_hbm, w_hbm, bias_ref, ids_ref, mine_ref, theirs_ref, out_ref, x_buf, w_buf, acc_ref, picked_ref, ids_buf, x_sem, w_sem
):
    layers, blocks, block, rows = x_buf.shape
    depth, feats = w_buf.shape[1:]
    slots = ids_ref.shape[0]

    def x_copy(layer, piece):
        part = pl.ds(piece * X_PIECE, X_PIECE)
        return pltpu.make_async_copy(x_hbm.at[part, layer], x_buf.at[layer, part], x_sem.at[layer, piece])

    def w_copy(layer, piece):
        part = pl.ds(piece * W_PIECE * block, W_PIECE * block)
        return pltpu.make_async_copy(w_hbm.at[layer, part], w_buf.at[layer, part], w_sem.at[layer, piece])

    queue, needs = [], []
    for layer in range(layers):
        done_x = done_w = 0
        for chunk in range(len(CHUNKS[layer])):
            end = sum(CHUNKS[layer][:chunk + 1])
            need = []
            while done_x * X_PIECE < end:
                need.append(x_copy(layer, done_x))
                done_x += 1
            while done_w * W_PIECE < end:
                need.append(w_copy(layer, done_w))
                done_w += 1
            queue += need
            needs.append(need)

    def start_next():
        if queue:
            queue.pop(0).start()

    for _ in range(AHEAD):
        start_next()

    def pick(point):
        pick_scores(ids_ref, mine_ref, theirs_ref, picked_ref, ids_buf, PICKS[point])

    pick(0)
    lane = lax.broadcasted_iota(jnp.int32, (rows, LANES), 1)
    for layer in range(layers):
        for chunk, count in enumerate(CHUNKS[layer]):
            for copy in needs.pop(0):
                copy.wait()
                start_next()
            start = sum(CHUNKS[layer][:chunk])
            product = lax.dot_general(
                x_buf[layer, start:start + count].reshape(count * block, rows),
                w_buf[layer, start * block:(start + count) * block],
                (((0,), (0,)), ((), ())),
                preferred_element_type=jnp.float32,
            )
            if chunk == 0:
                acc_ref[...] = product + bias_ref[layer:layer + 1, :]
            else:
                acc_ref[...] += product

        pick(layer + 1)
        loc = local_slots(ids_ref, ids_buf, layer)
        lo = loc & (LANES - 1)
        group = loc >> 7
        act = jnp.zeros((rows, LANES), jnp.float32)
        for g in range(feats // LANES):
            got = jnp.take_along_axis(acc_ref[:, g * LANES:(g + 1) * LANES], lo, axis=1)
            act = jnp.where(group == g, got, act)
        for j in range(slots // 2):
            columns = slice(j * LANES, (j + 1) * LANES)
            value = jnp.take_along_axis(act, 2 * j + (lane >> 6), axis=1)
            edges = (value * picked_ref[layer, :, columns].astype(jnp.float32)).astype(out_ref.dtype)
            out_ref[:, layer, :, columns] = edges.reshape(blocks, rows // blocks, LANES)


def local_slots(ids_ref, ids_buf, layer):
    slots = ids_ref.shape[0]
    ids_buf[...] = jnp.full_like(ids_buf, -1)
    ids_buf[:slots, :] = ids_ref[:, layer, :]
    ids = ids_buf[...].T
    return jnp.where(ids >= 0, ids - lax.axis_index("feat") * FEATS, -1)


def pick_scores(ids_ref, mine_ref, theirs_ref, picked_ref, ids_buf, which):
    slots, layers, rows = ids_ref.shape
    targets, feats = mine_ref.shape
    core = lax.axis_index("tok") % 2
    lane = lax.broadcasted_iota(jnp.int32, (rows, LANES), 1)
    lower = lane < targets
    width = 2 * LANES
    for layer in which:
        loc = local_slots(ids_ref, ids_buf, layer)
        table = jnp.where(core == layer, mine_ref[...], theirs_ref[...])
        rhs = jnp.concatenate([table[:, h * width:(h + 1) * width] for h in range(feats // width)], 0)
        for j in range(slots // 2):
            halves = []
            for k in (2 * j, 2 * j + 1):
                here = jnp.take_along_axis(loc, jnp.full((rows, LANES), k, jnp.int32), axis=1)
                low = here & (width - 1)
                onehot = jnp.concatenate(
                    [jnp.where(low == lane + part * LANES, 1.0, 0.0).astype(table.dtype) for part in range(2)], 1
                )
                found = lax.dot_general(
                    onehot, rhs, (((1,), (1,)), ((), ())), preferred_element_type=jnp.float32
                )
                quarter = here >> 8
                two = jnp.where(quarter < 2, found[:, :LANES], found[:, LANES:])
                turned = pltpu.roll(two, targets, 1)
                halves.append(jnp.where((quarter & 1) == k % 2, two, turned))
            picked = jnp.where(lower, halves[0], halves[1])
            picked_ref[layer, :, j * LANES:(j + 1) * LANES] = picked.astype(picked_ref.dtype)


def make_edges(x, weight, bias, ids, mine, theirs):
    blocks, layers, block, rows = x.shape
    depth, feats = weight.shape[1:]
    columns = ids.shape[0] * mine.shape[0]
    vmem = pl.BlockSpec(memory_space=pltpu.VMEM)
    hbm = pl.BlockSpec(memory_space=pl.ANY)
    return pl.pallas_call(
        edge_kernel,
        in_specs=[hbm, hbm, vmem, vmem, vmem, vmem],
        out_specs=vmem,
        out_shape=jax.ShapeDtypeStruct((blocks, layers, rows // blocks, columns), jnp.bfloat16),
        scratch_shapes=[
            pltpu.VMEM((layers, blocks, block, rows), x.dtype),
            pltpu.VMEM((layers, depth, feats), weight.dtype),
            pltpu.VMEM((rows, feats), jnp.float32),
            pltpu.VMEM((layers, rows, columns), mine.dtype),
            pltpu.VMEM((LANES, rows), jnp.int32),
            pltpu.SemaphoreType.DMA((layers, blocks // X_PIECE)),
            pltpu.SemaphoreType.DMA((layers, blocks // W_PIECE)),
        ],
        compiler_params=pltpu.CompilerParams(vmem_limit_bytes=EDGE_VMEM),
        cost_estimate=pl.CostEstimate(
            flops=2 * layers * rows * depth * feats,
            bytes_accessed=2 * layers * depth * (feats + rows),
            transcendentals=0,
        ),
        name="edges",
    )(x, weight, bias, ids, mine, theirs)


def partner_of(axis, flip):
    pairs = []
    for i in range(128):
        tok, feat = divmod(i, 16)
        place = {"z": tok // 2, "core": tok % 2, "x": feat // 4, "y": feat % 4}
        place[axis] ^= flip
        pairs.append((i, (place["z"] * 2 + place["core"]) * 16 + place["x"] * 4 + place["y"]))
    return pairs


def swap(value, axis, flip):
    return lax.ppermute(value, ("tok", "feat"), partner_of(axis, flip))


def per_device(residual, enc_weight, enc_bias, dec_sum, unembed, norm_gain, target_ids, active_ids):
    n_tok = lax.axis_size("tok")
    n_feat = lax.axis_size("feat")
    tok_pos = lax.axis_index("tok")
    core = tok_pos % 2
    layers, rows, _ = residual.shape
    targets = target_ids.shape[0]
    slots = active_ids.shape[2]

    x = lax.all_gather(residual.transpose(0, 2, 1), "feat", axis=0, tiled=False)

    keep, send = owned_rows(target_ids, unembed, norm_gain, n_tok)
    keep = keep + swap(send, "core", 1)
    keep = keep[:2] + swap(keep[:1:-1], "z", 3)
    part = keep[0] + swap(keep[1], "z", 1)
    for axis, flip in (("x", 1), ("x", 3), ("y", 1), ("y", 3)):
        part = part + swap(part, axis, flip)

    terms = jnp.einsum("td,lfd->ltf", part, dec_sum, preferred_element_type=jnp.float32)
    own = lax.dynamic_index_in_dim(terms, core, 0, keepdims=False)
    other = lax.dynamic_index_in_dim(terms, 1 - core, 0, keepdims=False)
    total = own + swap(other, "core", 1)
    for flip in (3, 1):
        total = total + swap(total.astype(jnp.bfloat16), "z", flip).astype(jnp.float32)
    mine = total.astype(jnp.bfloat16)
    theirs = swap(mine, "core", 1)

    ids = active_ids.transpose(2, 0, 1)
    edges = make_edges(x, enc_weight, enc_bias, ids, mine, theirs)
    edges = lax.all_to_all(edges, "feat", split_axis=0, concat_axis=0, tiled=True)
    return edges.transpose(1, 2, 0, 3).reshape(layers, rows // n_feat, n_feat * slots * targets)


def solution(mesh):
    return jax.shard_map(
        per_device,
        mesh=mesh,
        in_specs=(
            P(None, "tok", "feat"),
            P(None, None, "feat"),
            P(None, "feat"),
            P(None, "feat", "tok"),
            P(("tok", "feat"), None),
            P(),
            P(),
            P(None, "tok", "feat"),
        ),
        out_specs=P(None, ("tok", "feat"), None),
        check_vma=False,
    )
```

```python
import jax
import jax.numpy as jnp
from jax import lax
from jax.experimental import pallas as pl
from jax.experimental.pallas import tpu as pltpu
from jax.sharding import PartitionSpec as P


LANES = 128
CHUNKS = ((4, 4, 8), (8, 8))
X_PIECE = 4
W_PIECE = 4
AHEAD = 16
PICKS = ((0,), (1,), ())
FEATS = 1024
EDGE_VMEM = 52 * 2**20
ROWS_VMEM = 50 * 2**20


def owned_rows_kernel(ids_ref, unembed_hbm, keep_ref, send_ref, tile_buf, row_buf, found_ref, count_ref, sem):
    targets = ids_ref.shape[0]
    tile = tile_buf.shape[1]
    count = unembed_hbm.shape[0]
    tok = lax.axis_index("tok")
    first = (tok * lax.axis_size("feat") + lax.axis_index("feat")) * count
    z, core = tok // 2, tok % 2

    def copy(i):
        row = ids_ref[i] - first
        start = pl.multiple_of(lax.shift_right_logical(row, 3) * tile, tile)
        return pltpu.make_async_copy(unembed_hbm.at[pl.ds(start, tile)], tile_buf.at[i], sem.at[i])

    count_ref[0] = 0

    @pl.loop(0, targets, unroll=8)
    def _(i):
        row = ids_ref[i] - first

        @pl.when(jnp.logical_and(row >= 0, row < count))
        def _():
            copy(i).start()
            found_ref[count_ref[0]] = i
            count_ref[0] += 1

    row_buf[...] = jnp.zeros_like(row_buf)

    @pl.loop(0, count_ref[0])
    def _(n):
        i = found_ref[n]
        copy(i).wait()
        rows = tile_buf[i].astype(jnp.float32)
        wanted = (ids_ref[i] - first) & (tile - 1)
        here = lax.broadcasted_iota(jnp.int32, rows.shape, 0) == wanted
        row_buf[pl.ds(i, 1), :] = jnp.sum(jnp.where(here, rows, 0.0), axis=0, keepdims=True)

    zs, _, width = keep_ref.shape
    for part in range(2 * zs):
        value = row_buf[:, part * width:(part + 1) * width].astype(keep_ref.dtype)
        slot = z ^ (part // 2)

        @pl.when(core == part % 2)
        def _(value=value, slot=slot):
            keep_ref[slot] = value

        @pl.when(core != part % 2)
        def _(value=value, slot=slot):
            send_ref[slot] = value


def owned_rows(target_ids, unembed, parts):
    targets = target_ids.shape[0]
    depth = unembed.shape[1]
    smem = pl.BlockSpec(memory_space=pltpu.SMEM)
    vmem = pl.BlockSpec(memory_space=pltpu.VMEM)
    shape = jax.ShapeDtypeStruct((parts // 2, targets, depth // parts), jnp.bfloat16)
    return pl.pallas_call(
        owned_rows_kernel,
        in_specs=[smem, pl.BlockSpec(memory_space=pl.ANY)],
        out_specs=[vmem, vmem],
        out_shape=[shape, shape],
        scratch_shapes=[
            pltpu.VMEM((targets, 8, depth), unembed.dtype),
            pltpu.VMEM((targets, depth), jnp.float32),
            pltpu.SMEM((targets,), jnp.int32),
            pltpu.SMEM((1,), jnp.int32),
            pltpu.SemaphoreType.DMA((targets,)),
        ],
        compiler_params=pltpu.CompilerParams(vmem_limit_bytes=ROWS_VMEM),
        name="owned_rows",
    )(target_ids, unembed)


def edge_kernel(
    x_hbm, w_hbm, bias_ref, ids_ref, mine_ref, theirs_ref, out_ref, x_buf, w_buf, acc_ref, picked_ref, ids_buf, x_sem, w_sem
):
    layers, blocks, block, rows = x_buf.shape
    depth, feats = w_buf.shape[1:]
    slots = ids_ref.shape[0]

    def x_copy(layer, piece):
        part = pl.ds(piece * X_PIECE, X_PIECE)
        return pltpu.make_async_copy(x_hbm.at[part, layer], x_buf.at[layer, part], x_sem.at[layer, piece])

    def w_copy(layer, piece):
        part = pl.ds(piece * W_PIECE * block, W_PIECE * block)
        return pltpu.make_async_copy(w_hbm.at[layer, part], w_buf.at[layer, part], w_sem.at[layer, piece])

    queue, needs = [], []
    for layer in range(layers):
        done_x = done_w = 0
        for chunk in range(len(CHUNKS[layer])):
            end = sum(CHUNKS[layer][:chunk + 1])
            need = []
            while done_x * X_PIECE < end:
                need.append(x_copy(layer, done_x))
                done_x += 1
            while done_w * W_PIECE < end:
                need.append(w_copy(layer, done_w))
                done_w += 1
            queue += need
            needs.append(need)

    def start_next():
        if queue:
            queue.pop(0).start()

    for _ in range(AHEAD):
        start_next()

    def pick(point):
        pick_scores(ids_ref, mine_ref, theirs_ref, picked_ref, ids_buf, PICKS[point])

    pick(0)
    lane = lax.broadcasted_iota(jnp.int32, (rows, LANES), 1)
    for layer in range(layers):
        for chunk, count in enumerate(CHUNKS[layer]):
            for copy in needs.pop(0):
                copy.wait()
                start_next()
            start = sum(CHUNKS[layer][:chunk])
            product = lax.dot_general(
                x_buf[layer, start:start + count].reshape(count * block, rows),
                w_buf[layer, start * block:(start + count) * block],
                (((0,), (0,)), ((), ())),
                preferred_element_type=jnp.float32,
            )
            if chunk == 0:
                acc_ref[...] = product + bias_ref[layer:layer + 1, :]
            else:
                acc_ref[...] += product

        pick(layer + 1)
        loc = local_slots(ids_ref, ids_buf, layer)
        lo = loc & (LANES - 1)
        group = loc >> 7
        act = jnp.zeros((rows, LANES), jnp.float32)
        for g in range(feats // LANES):
            got = jnp.take_along_axis(acc_ref[:, g * LANES:(g + 1) * LANES], lo, axis=1)
            act = jnp.where(group == g, got, act)
        for j in range(slots // 2):
            columns = slice(j * LANES, (j + 1) * LANES)
            value = jnp.take_along_axis(act, 2 * j + (lane >> 6), axis=1)
            edges = (value * picked_ref[layer, :, columns].astype(jnp.float32)).astype(out_ref.dtype)
            out_ref[:, layer, :, columns] = edges.reshape(blocks, rows // blocks, LANES)


def local_slots(ids_ref, ids_buf, layer):
    slots = ids_ref.shape[0]
    ids_buf[...] = jnp.full_like(ids_buf, -1)
    ids_buf[:slots, :] = ids_ref[:, layer, :]
    ids = ids_buf[...].T
    return jnp.where(ids >= 0, ids - lax.axis_index("feat") * FEATS, -1)


def pick_scores(ids_ref, mine_ref, theirs_ref, picked_ref, ids_buf, which):
    slots, layers, rows = ids_ref.shape
    targets, feats = mine_ref.shape
    core = lax.axis_index("tok") % 2
    lane = lax.broadcasted_iota(jnp.int32, (rows, LANES), 1)
    lower = lane < targets
    width = 2 * LANES
    for layer in which:
        loc = local_slots(ids_ref, ids_buf, layer)
        table = jnp.where(core == layer, mine_ref[...], theirs_ref[...])
        rhs = jnp.concatenate([table[:, h * width:(h + 1) * width] for h in range(feats // width)], 0)
        for j in range(slots // 2):
            halves = []
            for k in (2 * j, 2 * j + 1):
                here = jnp.take_along_axis(loc, jnp.full((rows, LANES), k, jnp.int32), axis=1)
                low = here & (width - 1)
                onehot = jnp.concatenate(
                    [jnp.where(low == lane + part * LANES, 1.0, 0.0).astype(table.dtype) for part in range(2)], 1
                )
                found = lax.dot_general(
                    onehot, rhs, (((1,), (1,)), ((), ())), preferred_element_type=jnp.float32
                )
                quarter = here >> 8
                two = jnp.where(quarter < 2, found[:, :LANES], found[:, LANES:])
                turned = pltpu.roll(two, targets, 1)
                halves.append(jnp.where((quarter & 1) == k % 2, two, turned))
            picked = jnp.where(lower, halves[0], halves[1])
            picked_ref[layer, :, j * LANES:(j + 1) * LANES] = picked.astype(picked_ref.dtype)


def make_edges(x, weight, bias, ids, mine, theirs):
    blocks, layers, block, rows = x.shape
    depth, feats = weight.shape[1:]
    columns = ids.shape[0] * mine.shape[0]
    vmem = pl.BlockSpec(memory_space=pltpu.VMEM)
    hbm = pl.BlockSpec(memory_space=pl.ANY)
    return pl.pallas_call(
        edge_kernel,
        in_specs=[hbm, hbm, vmem, vmem, vmem, vmem],
        out_specs=vmem,
        out_shape=jax.ShapeDtypeStruct((blocks, layers, rows // blocks, columns), jnp.bfloat16),
        scratch_shapes=[
            pltpu.VMEM((layers, blocks, block, rows), x.dtype),
            pltpu.VMEM((layers, depth, feats), weight.dtype),
            pltpu.VMEM((rows, feats), jnp.float32),
            pltpu.VMEM((layers, rows, columns), mine.dtype),
            pltpu.VMEM((LANES, rows), jnp.int32),
            pltpu.SemaphoreType.DMA((layers, blocks // X_PIECE)),
            pltpu.SemaphoreType.DMA((layers, blocks // W_PIECE)),
        ],
        compiler_params=pltpu.CompilerParams(vmem_limit_bytes=EDGE_VMEM),
        cost_estimate=pl.CostEstimate(
            flops=2 * layers * rows * depth * feats,
            bytes_accessed=2 * layers * depth * (feats + rows),
            transcendentals=0,
        ),
        name="edges",
    )(x, weight, bias, ids, mine, theirs)


def partner_of(axis, flip):
    pairs = []
    for i in range(128):
        tok, feat = divmod(i, 16)
        place = {"z": tok // 2, "core": tok % 2, "x": feat // 4, "y": feat % 4}
        place[axis] ^= flip
        pairs.append((i, (place["z"] * 2 + place["core"]) * 16 + place["x"] * 4 + place["y"]))
    return pairs


def swap(value, axis, flip):
    return lax.ppermute(value, ("tok", "feat"), partner_of(axis, flip))


def per_device(residual, enc_weight, enc_bias, dec_sum, unembed, norm_gain, target_ids, active_ids):
    n_tok = lax.axis_size("tok")
    n_feat = lax.axis_size("feat")
    tok_pos = lax.axis_index("tok")
    core = tok_pos % 2
    layers, rows, _ = residual.shape
    targets = target_ids.shape[0]
    slots = active_ids.shape[2]

    x = lax.all_gather(residual.transpose(0, 2, 1), "feat", axis=0, tiled=False)

    keep, send = owned_rows(target_ids, unembed, n_tok)
    keep = keep + swap(send, "core", 1)
    keep = keep[:2] + swap(keep[:1:-1], "z", 3)
    part = keep[0] + swap(keep[1], "z", 1)
    for axis in ("x", "y"):
        others = [swap(part, axis, flip) for flip in (1, 3, 2)]
        part = (part + others[0]) + (others[1] + others[2])

    gain = lax.dynamic_slice_in_dim(norm_gain, tok_pos * part.shape[1], part.shape[1])
    directions = (part.astype(jnp.float32) * gain[None, :]).astype(jnp.bfloat16)
    terms = jnp.einsum("td,lfd->ltf", directions, dec_sum, preferred_element_type=jnp.float32)
    own = lax.dynamic_index_in_dim(terms, core, 0, keepdims=False)
    other = lax.dynamic_index_in_dim(terms, 1 - core, 0, keepdims=False)
    total = own + swap(other, "core", 1)
    for flip in (3, 1):
        total = total + swap(total.astype(jnp.bfloat16), "z", flip).astype(jnp.float32)
    mine = total.astype(jnp.bfloat16)
    theirs = swap(mine, "core", 1)

    ids = active_ids.transpose(2, 0, 1)
    edges = make_edges(x, enc_weight, enc_bias, ids, mine, theirs)
    edges = lax.all_to_all(edges, "feat", split_axis=0, concat_axis=0, tiled=True)
    return edges.transpose(1, 2, 0, 3).reshape(layers, rows // n_feat, n_feat * slots * targets)


def solution(mesh):
    return jax.shard_map(
        per_device,
        mesh=mesh,
        in_specs=(
            P(None, "tok", "feat"),
            P(None, None, "feat"),
            P(None, "feat"),
            P(None, "feat", "tok"),
            P(("tok", "feat"), None),
            P(),
            P(),
            P(None, "tok", "feat"),
        ),
        out_specs=P(None, ("tok", "feat"), None),
        check_vma=False,
    )
```

```python
import jax
import jax.numpy as jnp
from jax import lax
from jax.experimental import pallas as pl
from jax.experimental.pallas import tpu as pltpu
from jax.sharding import PartitionSpec as P


LANES = 128
CHUNKS = ((8, 8), (8, 8))
X_PIECE = 4
W_PIECE = 4
AHEAD = 16
EARLY_LAYER = 0
FEATS = 1024
EDGE_VMEM = 52 * 2**20
ROWS_VMEM = 50 * 2**20


def owned_rows_kernel(ids_ref, unembed_hbm, keep_ref, send_ref, tile_buf, row_buf, found_ref, count_ref, sem):
    targets = ids_ref.shape[0]
    tile = tile_buf.shape[1]
    count = unembed_hbm.shape[0]
    tok = lax.axis_index("tok")
    first = (tok * lax.axis_size("feat") + lax.axis_index("feat")) * count
    z, core = tok // 2, tok % 2

    def copy(i):
        row = ids_ref[i] - first
        start = pl.multiple_of(lax.shift_right_logical(row, 3) * tile, tile)
        return pltpu.make_async_copy(unembed_hbm.at[pl.ds(start, tile)], tile_buf.at[i], sem.at[i])

    count_ref[0] = 0

    @pl.loop(0, targets, unroll=8)
    def _(i):
        row = ids_ref[i] - first

        @pl.when(jnp.logical_and(row >= 0, row < count))
        def _():
            copy(i).start()
            found_ref[count_ref[0]] = i
            count_ref[0] += 1

    row_buf[...] = jnp.zeros_like(row_buf)

    @pl.loop(0, count_ref[0])
    def _(n):
        i = found_ref[n]
        copy(i).wait()
        rows = tile_buf[i].astype(jnp.float32)
        wanted = (ids_ref[i] - first) & (tile - 1)
        here = lax.broadcasted_iota(jnp.int32, rows.shape, 0) == wanted
        row_buf[pl.ds(i, 1), :] = jnp.sum(jnp.where(here, rows, 0.0), axis=0, keepdims=True)

    zs, _, width = keep_ref.shape
    for part in range(2 * zs):
        value = row_buf[:, part * width:(part + 1) * width].astype(keep_ref.dtype)
        slot = z ^ (part // 2)

        @pl.when(core == part % 2)
        def _(value=value, slot=slot):
            keep_ref[slot] = value

        @pl.when(core != part % 2)
        def _(value=value, slot=slot):
            send_ref[slot] = value


def owned_rows(target_ids, unembed, parts):
    targets = target_ids.shape[0]
    depth = unembed.shape[1]
    smem = pl.BlockSpec(memory_space=pltpu.SMEM)
    vmem = pl.BlockSpec(memory_space=pltpu.VMEM)
    shape = jax.ShapeDtypeStruct((parts // 2, targets, depth // parts), jnp.bfloat16)
    return pl.pallas_call(
        owned_rows_kernel,
        in_specs=[smem, pl.BlockSpec(memory_space=pl.ANY)],
        out_specs=[vmem, vmem],
        out_shape=[shape, shape],
        scratch_shapes=[
            pltpu.VMEM((targets, 8, depth), unembed.dtype),
            pltpu.VMEM((targets, depth), jnp.float32),
            pltpu.SMEM((targets,), jnp.int32),
            pltpu.SMEM((1,), jnp.int32),
            pltpu.SemaphoreType.DMA((targets,)),
        ],
        compiler_params=pltpu.CompilerParams(vmem_limit_bytes=ROWS_VMEM),
        name="owned_rows",
    )(target_ids, unembed)


def edge_kernel(
    x_hbm, w_hbm, bias_ref, ids_ref, mine_ref, theirs_ref, early_ref, out_ref, x_buf, w_buf, acc_ref, late_ref, ids_buf, x_sem, w_sem
):
    layers, blocks, block, rows = x_buf.shape
    depth, feats = w_buf.shape[1:]
    slots = ids_ref.shape[0]

    def x_copy(layer, piece):
        part = pl.ds(piece * X_PIECE, X_PIECE)
        return pltpu.make_async_copy(x_hbm.at[part, layer], x_buf.at[layer, part], x_sem.at[layer, piece])

    def w_copy(layer, piece):
        part = pl.ds(piece * W_PIECE * block, W_PIECE * block)
        return pltpu.make_async_copy(w_hbm.at[layer, part], w_buf.at[layer, part], w_sem.at[layer, piece])

    queue, needs = [], []
    for layer in range(layers):
        done_x = done_w = 0
        for chunk in range(len(CHUNKS[layer])):
            end = sum(CHUNKS[layer][:chunk + 1])
            need = []
            while done_x * X_PIECE < end:
                need.append(x_copy(layer, done_x))
                done_x += 1
            while done_w * W_PIECE < end:
                need.append(w_copy(layer, done_w))
                done_w += 1
            queue += need
            needs.append(need)

    def start_next():
        if queue:
            queue.pop(0).start()

    for _ in range(AHEAD):
        start_next()

    for layer in range(layers):
        if layer != EARLY_LAYER:
            pick_scores(layer, ids_ref, mine_ref, theirs_ref, late_ref, ids_buf)
    lane = lax.broadcasted_iota(jnp.int32, (rows, LANES), 1)
    for layer in range(layers):
        for chunk, count in enumerate(CHUNKS[layer]):
            for copy in needs.pop(0):
                copy.wait()
                start_next()
            start = sum(CHUNKS[layer][:chunk])
            product = lax.dot_general(
                x_buf[layer, start:start + count].reshape(count * block, rows),
                w_buf[layer, start * block:(start + count) * block],
                (((0,), (0,)), ((), ())),
                preferred_element_type=jnp.float32,
            )
            if chunk == 0:
                acc_ref[...] = product + bias_ref[layer:layer + 1, :]
            else:
                acc_ref[...] += product

        picked_ref = early_ref if layer == EARLY_LAYER else late_ref
        loc = local_slots(ids_ref, ids_buf, layer)
        lo = loc & (LANES - 1)
        group = loc >> 7
        act = jnp.zeros((rows, LANES), jnp.float32)
        for g in range(feats // LANES):
            got = jnp.take_along_axis(acc_ref[:, g * LANES:(g + 1) * LANES], lo, axis=1)
            act = jnp.where(group == g, got, act)
        for j in range(slots // 2):
            columns = slice(j * LANES, (j + 1) * LANES)
            value = jnp.take_along_axis(act, 2 * j + (lane >> 6), axis=1)
            edges = (value * picked_ref[:, columns].astype(jnp.float32)).astype(out_ref.dtype)
            out_ref[:, layer, :, columns] = edges.reshape(blocks, rows // blocks, LANES)


def local_slots(ids_ref, ids_buf, layer):
    slots = ids_ref.shape[0]
    ids_buf[...] = jnp.full_like(ids_buf, -1)
    ids_buf[:slots, :] = ids_ref[:, layer, :]
    ids = ids_buf[...].T
    return jnp.where(ids >= 0, ids - lax.axis_index("feat") * FEATS, -1)


def pick_scores(layer, ids_ref, mine_ref, theirs_ref, picked_ref, ids_buf):
    slots, _, rows = ids_ref.shape
    targets, feats = mine_ref.shape
    core = lax.axis_index("tok") % 2
    lane = lax.broadcasted_iota(jnp.int32, (rows, LANES), 1)
    lower = lane < targets
    width = 2 * LANES
    loc = local_slots(ids_ref, ids_buf, layer)
    table = jnp.where(core == layer, mine_ref[...], theirs_ref[...])
    rhs = jnp.concatenate([table[:, h * width:(h + 1) * width] for h in range(feats // width)], 0)
    for j in range(slots // 2):
        halves = []
        for k in (2 * j, 2 * j + 1):
            here = jnp.take_along_axis(loc, jnp.full((rows, LANES), k, jnp.int32), axis=1)
            low = here & (width - 1)
            onehot = jnp.concatenate(
                [jnp.where(low == lane + part * LANES, 1.0, 0.0).astype(table.dtype) for part in range(2)], 1
            )
            found = lax.dot_general(
                onehot, rhs, (((1,), (1,)), ((), ())), preferred_element_type=jnp.float32
            )
            quarter = here >> 8
            two = jnp.where(quarter < 2, found[:, :LANES], found[:, LANES:])
            turned = pltpu.roll(two, targets, 1)
            halves.append(jnp.where((quarter & 1) == k % 2, two, turned))
        picked = jnp.where(lower, halves[0], halves[1])
        picked_ref[:, j * LANES:(j + 1) * LANES] = picked.astype(picked_ref.dtype)


def pick_early(ids, mine, theirs):
    slots, _, rows = ids.shape
    vmem = pl.BlockSpec(memory_space=pltpu.VMEM)
    return pl.pallas_call(
        lambda *refs: pick_scores(EARLY_LAYER, *refs),
        in_specs=[vmem, vmem, vmem],
        out_specs=vmem,
        out_shape=jax.ShapeDtypeStruct((rows, slots * mine.shape[0]), mine.dtype),
        scratch_shapes=[pltpu.VMEM((LANES, rows), jnp.int32)],
        compiler_params=pltpu.CompilerParams(vmem_limit_bytes=EDGE_VMEM),
        name="pick_early",
    )(ids, mine, theirs)


def make_edges(x, weight, bias, ids, mine, theirs, early):
    blocks, layers, block, rows = x.shape
    depth, feats = weight.shape[1:]
    columns = ids.shape[0] * mine.shape[0]
    vmem = pl.BlockSpec(memory_space=pltpu.VMEM)
    hbm = pl.BlockSpec(memory_space=pl.ANY)
    return pl.pallas_call(
        edge_kernel,
        in_specs=[hbm, hbm, vmem, vmem, vmem, vmem, vmem],
        out_specs=vmem,
        out_shape=jax.ShapeDtypeStruct((blocks, layers, rows // blocks, columns), jnp.bfloat16),
        scratch_shapes=[
            pltpu.VMEM((layers, blocks, block, rows), x.dtype),
            pltpu.VMEM((layers, depth, feats), weight.dtype),
            pltpu.VMEM((rows, feats), jnp.float32),
            pltpu.VMEM((rows, columns), mine.dtype),
            pltpu.VMEM((LANES, rows), jnp.int32),
            pltpu.SemaphoreType.DMA((layers, blocks // X_PIECE)),
            pltpu.SemaphoreType.DMA((layers, blocks // W_PIECE)),
        ],
        compiler_params=pltpu.CompilerParams(vmem_limit_bytes=EDGE_VMEM),
        cost_estimate=pl.CostEstimate(
            flops=2 * layers * rows * depth * feats,
            bytes_accessed=2 * layers * depth * (feats + rows),
            transcendentals=0,
        ),
        name="edges",
    )(x, weight, bias, ids, mine, theirs, early)


def partner_of(axis, flip):
    pairs = []
    for i in range(128):
        tok, feat = divmod(i, 16)
        place = {"z": tok // 2, "core": tok % 2, "x": feat // 4, "y": feat % 4}
        place[axis] ^= flip
        pairs.append((i, (place["z"] * 2 + place["core"]) * 16 + place["x"] * 4 + place["y"]))
    return pairs


def swap(value, axis, flip):
    return lax.ppermute(value, ("tok", "feat"), partner_of(axis, flip))


def per_device(residual, enc_weight, enc_bias, dec_sum, unembed, norm_gain, target_ids, active_ids):
    n_tok = lax.axis_size("tok")
    n_feat = lax.axis_size("feat")
    tok_pos = lax.axis_index("tok")
    core = tok_pos % 2
    layers, rows, _ = residual.shape
    targets = target_ids.shape[0]
    slots = active_ids.shape[2]

    x = lax.all_gather(residual.transpose(0, 2, 1), "feat", axis=0, tiled=False)

    keep, send = owned_rows(target_ids, unembed, n_tok)
    keep = keep + swap(send, "core", 1)
    keep = keep[:2] + swap(keep[:1:-1], "z", 3)
    part = keep[0] + swap(keep[1], "z", 1)
    for axis in ("x", "y"):
        others = [swap(part, axis, flip) for flip in (1, 3, 2)]
        part = (part + others[0]) + (others[1] + others[2])

    gain = lax.dynamic_slice_in_dim(norm_gain, tok_pos * part.shape[1], part.shape[1])
    directions = (part.astype(jnp.float32) * gain[None, :]).astype(jnp.bfloat16)
    terms = jnp.einsum("td,lfd->ltf", directions, dec_sum, preferred_element_type=jnp.float32)
    own = lax.dynamic_index_in_dim(terms, core, 0, keepdims=False)
    other = lax.dynamic_index_in_dim(terms, 1 - core, 0, keepdims=False)
    total = own + swap(other, "core", 1)
    for flip in (3, 1):
        total = total + swap(total.astype(jnp.bfloat16), "z", flip).astype(jnp.float32)
    mine = total.astype(jnp.bfloat16)
    theirs = swap(mine, "core", 1)

    ids = active_ids.transpose(2, 0, 1)
    edges = make_edges(x, enc_weight, enc_bias, ids, mine, theirs, pick_early(ids, mine, theirs))
    edges = lax.all_to_all(edges, "feat", split_axis=0, concat_axis=0, tiled=True)
    return edges.transpose(1, 2, 0, 3).reshape(layers, rows // n_feat, n_feat * slots * targets)


def solution(mesh):
    return jax.shard_map(
        per_device,
        mesh=mesh,
        in_specs=(
            P(None, "tok", "feat"),
            P(None, None, "feat"),
            P(None, "feat"),
            P(None, "feat", "tok"),
            P(("tok", "feat"), None),
            P(),
            P(),
            P(None, "tok", "feat"),
        ),
        out_specs=P(None, ("tok", "feat"), None),
        check_vma=False,
    )
```
